32 devices in a mesh: depth: 2 (over x), mode: 2 (over y), tile: 8 (over z, core).
Axes of the slice: x: 2, y: 2, z: 4, core: 2. Of those that a mesh axis runs over, the one named last changes fastest.
Arguments:
- probe: float32 [2, 2, 256, 256], P('mode'), may hold values from -3 to 3
- object_slices: float32 [2, 2, 384, 2048], P('depth', None, None, 'tile'), may hold values from -4.2 to 4.2
- positions: int32 [16, 2], P('tile'), may hold values from 0 to 256, as said below
- measured: float32 [16, 256, 256], P('tile'), may hold values from 0 to 2
Outputs:
- object_gradient: float32 [2, 2, 384, 2048], P('depth', None, None, 'tile')
The draws below stay inside these ranges and needn't reach their ends.
Inputs may be any that keep to these rules, and one draw needn't show every extreme that they name: `positions`: position r belongs to tile r // 2. Entry 0 is its window's first row, at most 128; entry 1 is its first column counted in the tile's columns extended by 128 on each side, at most 256. Windows never leave the object: in the first tile the column entry is at least 128, in the last at most 128.
All inputs are finite; a program needn't handle non-finite values.
Results may differ from the reference program's by a relative error of at most 0.0003.
Values sent between devices are 32-bit elements; how exact they have to be, the bound alone decides.
A program may use at most 64 MiB of HBM per device.

```python
import math
import jax
import jax.numpy as jnp
from jax import lax

PROBE = 256
HALO = 128
TILE_X = 256
TILE_Y = 384
POS_DEV = 2
MODES = 2
SLICES = 2
POSITIONS = 16
OBJ_X = 2048


def draw_positions(key, part):
    count = POSITIONS
    tiles = POSITIONS // POS_DEV
    rows = jnp.arange(count, dtype=jnp.int32)
    owner = rows // POS_DEV
    lowest = jnp.where(owner == 0, HALO, 0)
    highest_col = jnp.where(owner == tiles - 1, HALO + TILE_X - PROBE, TILE_X + 2 * HALO - PROBE)
    key_rows = jax.random.fold_in(key, 11)
    key_cols = jax.random.fold_in(key, 23)
    top = jax.random.randint(key_rows, (count,), 0, TILE_Y - PROBE + 1, dtype=jnp.int32)
    spread = jax.random.randint(key_cols, (count,), 0, 1 << 20, dtype=jnp.int32)
    left = lowest + spread % (highest_col - lowest + 1)
    return jnp.stack([top, left], 1).astype(jnp.int32)


def block_scale(stream_key, dims, cuts, least, top_value):
    def one(dim, parts):
        heights = jax.random.uniform(jax.random.fold_in(jax.random.fold_in(stream_key, 6), dim), (parts,), jnp.float32, least / len(cuts), top_value / len(cuts))
        return jnp.repeat(jnp.exp(heights), dims[dim] // parts).reshape((-1,) + (1,) * (len(dims) - dim - 1))

    level = one(*cuts[0])
    for cut in cuts[1:]:
        level = level * one(*cut)
    return level


def bell_draw(own_key, extent, deviation, limit, split=(), kind=jnp.bfloat16):
    values = deviation * jax.random.normal(own_key, extent, jnp.float32)
    if split:
        values = values * block_scale(own_key, extent, split, -0.22, 0.18)
    return jnp.clip(values, -limit, limit).astype(kind)


def setup_inputs(seed: int = 0) -> dict:
    seeds = jax.random.split(jax.random.key(seed), 5)
    probe = bell_draw(seeds[0], (MODES, 2, PROBE, PROBE), 0.5, 3.0, ((0, 2),), jnp.float32)
    object_slices = bell_draw(seeds[1], (SLICES, 2, TILE_Y, OBJ_X), 0.7, 4.2, ((0, 2), (3, 8)), jnp.float32)
    positions = draw_positions(jax.random.fold_in(seeds[4], 71), 0)
    measured = jnp.clip(2.0 * jax.random.uniform(seeds[3], (POSITIONS, PROBE, PROBE), jnp.float32) ** block_scale(seeds[3], (POSITIONS, PROBE, PROBE), ((0, 8),), -0.2, 0.2), 0.0, 2.0)
    return {"probe": probe, "object_slices": object_slices, "positions": positions, "measured": measured}


def propagator(length):
    ordinal = jnp.arange(length, dtype=jnp.int32)
    signed = jnp.where(ordinal < length - length // 2, ordinal, ordinal - length)
    square = signed[:, None] * signed[:, None] + signed[None, :] * signed[None, :]
    angle = (-math.pi / (2.0 * length)) * ((3 * square) % (4 * length)).astype(jnp.float32)
    return lax.complex(jnp.cos(angle), jnp.sin(angle))


def reference(probe, object_slices, positions, measured):
    length = PROBE
    slices = object_slices.shape[0]
    transfer = propagator(length)
    extended = lax.complex(object_slices[:, 0], object_slices[:, 1])
    extended = jnp.pad(extended, ((0, 0), (0, 0), (HALO, HALO)))
    start_wave = lax.complex(probe[:, 0], probe[:, 1])
    zeros_real = jnp.zeros(extended.shape, jnp.float32)

    def visit(carry, entry):
        accum_r, accum_i = carry
        row_index, offset, pattern = entry
        owner = (row_index // POS_DEV).astype(jnp.int32)
        top = offset[0].astype(jnp.int32)
        column = (owner * TILE_X + offset[1]).astype(jnp.int32)
        start = (jnp.zeros((), jnp.int32), top, column)
        window = lax.dynamic_slice(extended, start, (slices, length, length))
        wave = start_wave
        inputs = []
        result = wave
        for layer_no in range(slices):
            inputs.append(wave)
            moved = wave * window[layer_no]
            result = jnp.fft.fft2(moved, norm="ortho")
            if layer_no + 1 < slices:
                wave = jnp.fft.ifft2(result * transfer, norm="ortho")
        intensity = jnp.sum(result.real * result.real + result.imag * result.imag, axis=0)
        grad = (intensity - pattern)[None] * result
        pieces = [None] * slices
        for layer_no in reversed(range(slices)):
            if layer_no == slices - 1:
                inner = jnp.fft.ifft2(grad, norm="ortho")
            else:
                inner = jnp.fft.ifft2(jnp.conj(transfer) * jnp.fft.fft2(grad, norm="ortho"), norm="ortho")
            pieces[layer_no] = jnp.sum(jnp.conj(inputs[layer_no]) * inner, axis=0)
            grad = jnp.conj(window[layer_no])[None] * inner
        stacked = jnp.stack(pieces, 0)
        current_r = lax.dynamic_slice(accum_r, start, (slices, length, length))
        current_i = lax.dynamic_slice(accum_i, start, (slices, length, length))
        accum_r = lax.dynamic_update_slice(accum_r, current_r + stacked.real, start)
        accum_i = lax.dynamic_update_slice(accum_i, current_i + stacked.imag, start)
        return (accum_r, accum_i), None

    rows = jnp.arange(positions.shape[0], dtype=jnp.int32)
    (accum_r, accum_i), unused = lax.scan(visit, (zeros_real, zeros_real), (rows, positions, measured))
    width = accum_r.shape[2] - 2 * HALO
    core_r = accum_r[:, :, HALO:HALO + width]
    core_i = accum_i[:, :, HALO:HALO + width]
    return jnp.stack([core_r, core_i], 1)
```

```python
import functools
import math

import jax
import jax.numpy as jnp
import numpy as np
from jax import lax
from jax.experimental import pallas as pl
from jax.experimental.pallas import tpu as pltpu
from jax.sharding import PartitionSpec as P

HALO = 128
MESH = pl.DeviceIdType.MESH


def split_table(table):
    high = table.astype(jnp.bfloat16)
    low = (table - high.astype(np.float64)).astype(jnp.bfloat16)
    return np.stack([high, low], 0)


def dft_tables(length):
    ordinal = np.arange(length)
    angle = 2.0 * math.pi / length * (ordinal[:, None] * ordinal[None, :] % length)
    cosine = np.cos(angle) / math.sqrt(length)
    sine = np.sin(angle) / math.sqrt(length)
    first = np.block([[cosine, -sine], [sine, cosine]])
    second = np.block([[cosine, sine], [-sine, cosine]])
    return np.stack([split_table(first), split_table(second)], 0)


def propagator(length):
    ordinal = np.arange(length)
    signed = np.where(ordinal < length - length // 2, ordinal, ordinal - length)
    square = signed[:, None] * signed[:, None] + signed[None, :] * signed[None, :]
    angle = -math.pi / (2.0 * length) * (3 * square % (4 * length))
    return np.stack([np.cos(angle), np.sin(angle)], 0).astype(np.float32)


def parts_of(value):
    high = value.astype(jnp.bfloat16)
    low = (value - high.astype(jnp.float32)).astype(jnp.bfloat16)
    return high, low


def mm(a, b):
    return jnp.dot(a, b, preferred_element_type=jnp.float32)


def transform(real, imag, tab, right, left):
    n = real.shape[0]
    high, low = parts_of(jnp.concatenate([real, imag], axis=1))
    half = mm(high, tab[right, 0]) + mm(low, tab[right, 0]) + mm(high, tab[right, 1])
    high, low = parts_of(jnp.concatenate([half[:, :n], half[:, n:]], axis=0))
    full = mm(tab[left, 0], high) + mm(tab[left, 0], low) + mm(tab[left, 1], high)
    return full[:n], full[n:]


def kernel(
    pairs,
    probe_ref,
    obj_ref,
    pos_ref,
    meas_ref,
    tab_hbm,
    prop_hbm,
    out_ref,
    ext_near,
    ext_far,
    psi0,
    psi1,
    win,
    pattern,
    posn,
    tab,
    prop,
    mine_int,
    their_int,
    vsend,
    vrecv,
    spread,
    accum,
    rim,
    load_sem,
    src_sem,
    fwd_sem,
    ext_sem,
    pos_sem,
    probe_sem,
    meas_sem,
    int_sem,
    v_sem,
    w_send,
    w_recv,
    rim_send,
    rim_recv,
    out_send,
    out_recv,
):
    n = psi0.shape[1]
    rows = obj_ref.shape[2]
    room = rows - n
    d = lax.axis_index("depth")
    m = lax.axis_index("mode")
    t = lax.axis_index("tile")
    c = lax.rem(t, 2)
    z = t // 2
    other = t + 1 - 2 * c
    own = 1 - (c - d) * (c - d)
    core = {"tile": other}
    across = {"depth": 1 - d}
    beside = {"mode": 1 - m}
    is_owner = c == d
    not_owner = c != d

    def rcopy(src, dst, send, recv, target):
        return pltpu.make_async_remote_copy(
            src_ref=src, dst_ref=dst, send_sem=send, recv_sem=recv, device_id=target, device_id_type=MESH
        )

    loads = [
        pltpu.make_async_copy(tab_hbm, tab, load_sem.at[0]),
        pltpu.make_async_copy(prop_hbm, prop, load_sem.at[1]),
    ]
    for item in loads:
        item.start()

    barrier = pltpu.get_barrier_semaphore()
    for target in (core, across, beside):
        pl.semaphore_signal(barrier, inc=1, device_id=target, device_id_type=MESH)

    @pl.when(z > 0)
    def _():
        for depth in (0, 1):
            pl.semaphore_signal(barrier, inc=1, device_id={"depth": depth, "tile": t - 2}, device_id_type=MESH)

    @pl.when(z < pairs - 1)
    def _():
        for depth in (0, 1):
            pl.semaphore_signal(barrier, inc=1, device_id={"depth": depth, "tile": t + 2}, device_id_type=MESH)

    peers = 3 + 2 * jnp.minimum(z, 1) + 2 * jnp.minimum(pairs - 1 - z, 1)
    pl.semaphore_wait(barrier, peers)

    ext = (ext_near, ext_far)

    def half_of(h):
        return obj_ref.at[0, :, :, pl.ds(pl.multiple_of(h * HALO, HALO), HALO)]

    def place(src, block, send, depth):
        for s in (0, 1):
            dst = ext[s].at[block]
            sem = ext_sem.at[s, block]

            @pl.when(jnp.logical_and(d == s, depth == s))
            def _():
                pltpu.make_async_copy(src, dst, sem).start()

            @pl.when(jnp.logical_and(d == s, depth != s))
            def _():
                rcopy(src, dst, send, sem, across).start()

    inner_block = 3 * c
    outer_block = 3 - 3 * c
    outer_tile = t - 2 + 4 * c
    has_outer = jnp.logical_or(jnp.logical_and(c == 0, z > 0), jnp.logical_and(c == 1, z < pairs - 1))

    def outer_copy(s):
        return rcopy(
            half_of(c),
            ext[s].at[outer_block],
            src_sem.at[3],
            ext_sem.at[s, outer_block],
            {"depth": 1 - c, "tile": outer_tile},
        )

    pos_copy = rcopy(pos_ref, posn, pos_sem.at[0], pos_sem.at[1], core)
    pos_copy.start()
    place(half_of(0), 1, src_sem.at[0], c)
    place(half_of(1), 2, src_sem.at[1], c)
    place(half_of(1 - c), inner_block, src_sem.at[2], 1 - c)

    for s in (0, 1):

        @pl.when(jnp.logical_and(has_outer, d == s))
        def _():
            outer_copy(s).start()

    probe_copy = rcopy(probe_ref.at[0], psi0, probe_sem.at[0], probe_sem.at[1], beside)

    @pl.when(c == m)
    def _():
        probe_copy.start()
        pltpu.make_async_copy(probe_ref.at[0], psi0, probe_sem.at[2]).start()

    meas_copy = rcopy(meas_ref.at[m], pattern, meas_sem.at[0], meas_sem.at[1], core)
    meas_local = pltpu.make_async_copy(meas_ref.at[m], pattern, meas_sem.at[2])

    @pl.when(is_owner)
    def _():
        meas_copy.start()
        meas_local.start()

    for s in (0, 1):
        ext[s][4] = jnp.zeros(ext_near.shape[1:], jnp.float32)

    no_left = jnp.logical_and(d == 0, z == 0)
    no_right = jnp.logical_and(d == 1, z == pairs - 1)

    @pl.when(no_left)
    def _():
        for s in (0, 1):
            ext[s][0] = jnp.zeros(ext_near.shape[1:], jnp.float32)

    @pl.when(no_right)
    def _():
        for s in (0, 1):
            ext[s][3] = jnp.zeros(ext_near.shape[1:], jnp.float32)

    @pl.when(is_owner)
    def _():
        @pl.loop(0, 4)
        def _(w):
            for j in (0, 1, 2, 5, 6):
                spread[w // 2, lax.rem(w, 2), j] = jnp.zeros(spread.shape[3:], jnp.float32)
            for j in (3, 4):
                for edge in (0, room + n):
                    spread[w // 2, lax.rem(w, 2), j, :, edge : edge + room, :] = jnp.zeros((2, room, HALO), jnp.float32)

    def ext_wait(s, block):
        rcopy(ext[s].at[block], ext[s].at[block], src_sem.at[0], ext_sem.at[s, block], core).wait_recv()

    def forward_copy(s, i, block):
        return rcopy(ext[s].at[block], ext[s].at[block], fwd_sem.at[s, i], ext_sem.at[s, block], core)

    def missing(i):
        return no_left if i == 0 else no_right

    def land(s):
        for i in (0, 1):

            @pl.when(is_owner)
            def _():
                ext_wait(s, 1 + i)
                forward_copy(s, i, 1 + i).start()

            @pl.when(jnp.logical_and(not_owner, jnp.logical_not(missing(i))))
            def _():
                ext_wait(s, 3 * i)
                forward_copy(s, i, 3 * i).start()

    def arrive(s):
        for i in (0, 1):

            @pl.when(not_owner)
            def _():
                ext_wait(s, 1 + i)

            @pl.when(jnp.logical_and(is_owner, jnp.logical_not(missing(i))))
            def _():
                ext_wait(s, 3 * i)

    lane = lax.broadcasted_iota(jnp.int32, (1, HALO), 1)

    def place_of(tile_no, which):
        mine = tile_no == c
        top = jnp.where(mine, pos_ref[which, 0], posn[which, 0])
        left = jnp.where(mine, pos_ref[which, 1], posn[which, 1])
        return top, left // HALO, lax.rem(left, HALO)

    def cut(s, spot):
        top, block, rem = spot
        back = lax.rem(HALO - rem, HALO)
        for part in (0, 1):
            for j in (0, 1):
                near = ext[s][block + j, part, pl.ds(top, n), :]
                far = ext[s][block + j + 1, part, pl.ds(top, n), :]
                mixed = jnp.where(lane >= rem, near, far)
                win[s, part, :, j * HALO : (j + 1) * HALO] = pltpu.roll(mixed, back, 1)

    @pl.when(d == 1)
    def _():
        land(1)

    land(0)
    for item in loads:
        item.wait()
    pos_copy.wait()

    @pl.when(c == m)
    def _():
        pltpu.make_async_copy(probe_ref.at[0], psi0, probe_sem.at[2]).wait()

    @pl.when(c != m)
    def _():
        probe_copy.wait_recv()

    spot = place_of(d, m)
    arrive(0)
    cut(0, spot)
    wr, wi = win[0, 0], win[0, 1]
    pr, pi = psi0[0], psi0[1]
    spec_r, spec_i = transform(pr * wr - pi * wi, pr * wi + pi * wr, tab, 0, 1)
    hr, hi = prop[0], prop[1]
    wave_r, wave_i = transform(spec_r * hr - spec_i * hi, spec_r * hi + spec_i * hr, tab, 1, 0)
    psi1[0] = wave_r
    psi1[1] = wave_i

    @pl.when(d == 0)
    def _():
        land(1)

    arrive(1)
    cut(1, spot)
    wr, wi = win[1, 0], win[1, 1]
    wave_r, wave_i = psi1[0], psi1[1]
    far_r, far_i = transform(wave_r * wr - wave_i * wi, wave_r * wi + wave_i * wr, tab, 0, 1)
    mine_int[...] = far_r * far_r + far_i * far_i
    int_copy = rcopy(mine_int, their_int, int_sem.at[0], int_sem.at[1], core)
    int_copy.start()

    @pl.when(is_owner)
    def _():
        meas_local.wait()

    @pl.when(not_owner)
    def _():
        meas_copy.wait_recv()

    int_copy.wait()
    resid = mine_int[...] + their_int[...] - pattern[...]
    q_r, q_i = transform(resid * far_r, resid * far_i, tab, 1, 0)

    v_copy = rcopy(vsend, vrecv, v_sem.at[0], v_sem.at[1], core)

    def store_window(ref, start, real, imag):
        for j in (0, 1):
            cols = slice(j * HALO, (j + 1) * HALO)
            ref[j, 0, :, :] = real[:, cols]
            ref[j, 1, :, :] = imag[:, cols]

    def window_at(tile_no, which):
        return spread.at[tile_no, which, 3:5, :, room : room + n, :]

    def keep(real, imag):
        store_window(window_at(d, m), 0, real, imag)

    def to_across():
        return rcopy(window_at(d, m), window_at(d, m), w_send.at[0], w_recv.at[0], across)

    def to_beside(which_tile, k):
        return rcopy(window_at(which_tile, m), window_at(which_tile, m), w_send.at[k], w_recv.at[k], beside)

    def finish():
        v_copy.wait_recv()
        here = window_at(d, m)
        here[...] = here[...] + vrecv[...]

        @pl.when(is_owner)
        def _():
            to_beside(d, 1).start()

        @pl.when(not_owner)
        def _():
            to_across().start()

    wr, wi = win[1, 0], win[1, 1]
    wave_r, wave_i = psi1[0], psi1[1]
    v_r = wave_r * q_r + wave_i * q_i
    v_i = wave_r * q_i - wave_i * q_r

    @pl.when(c == 0)
    def _():
        store_window(vsend, 0, v_r, v_i)
        v_copy.start()

    @pl.when(c == 1)
    def _():
        keep(v_r, v_i)

    spec_r, spec_i = transform(wr * q_r + wi * q_i, wr * q_i - wi * q_r, tab, 0, 1)

    @pl.when(c == 1)
    def _():
        finish()

    hr, hi = prop[0], prop[1]
    q_r, q_i = transform(spec_r * hr + spec_i * hi, spec_i * hr - spec_r * hi, tab, 1, 0)
    pr, pi = psi0[0], psi0[1]
    v_r = pr * q_r + pi * q_i
    v_i = pr * q_i - pi * q_r

    @pl.when(c == 1)
    def _():
        store_window(vsend, 0, v_r, v_i)
        v_copy.start()

    @pl.when(c == 0)
    def _():
        keep(v_r, v_i)
        finish()

    def placed(tile_no, which, block, part):
        top, first, rem = place_of(tile_no, which)
        at = block - first + 3
        near = spread[tile_no, which, at, part, pl.ds(room - top, rows), :]
        far = spread[tile_no, which, at - 1, part, pl.ds(room - top, rows), :]
        return pltpu.roll(jnp.where(lane < HALO - rem, near, far), rem, 1)

    def gather_block(block):
        for part in (0, 1):
            terms = []
            for tile_no in (0, 1):
                local = block - 2 * tile_no
                if 0 <= local < 4:
                    for which in (0, 1):
                        terms.append(placed(tile_no, which, local, part))
            accum[block, part] = functools.reduce(jnp.add, terms)

    def rim_copy(side):
        return rcopy(
            accum.at[5 * side],
            rim.at[1 - side],
            rim_send.at[side],
            rim_recv.at[1 - side],
            {"tile": t - 2 + 4 * side},
        )

    def out_copy(half):
        block = 1 + 2 * (1 - d) + half
        return rcopy(
            accum.at[block],
            out_ref.at[0, :, :, half * HALO : (half + 1) * HALO],
            out_send.at[half],
            out_recv.at[half],
            core,
        )

    has_low = z > 0
    has_high = z < pairs - 1

    @pl.when(is_owner)
    def _():
        arrived = rcopy(window_at(1 - d, m), window_at(1 - d, m), w_send.at[2], w_recv.at[0], across)
        arrived.wait_recv()
        to_beside(1 - d, 2).start()
        rcopy(window_at(d, 1 - m), window_at(d, 1 - m), w_send.at[1], w_recv.at[1], beside).wait_recv()
        rcopy(window_at(1 - d, 1 - m), window_at(1 - d, 1 - m), w_send.at[2], w_recv.at[2], beside).wait_recv()
        gather_block(0)

        @pl.when(has_low)
        def _():
            rim_copy(0).start()

        gather_block(5)

        @pl.when(has_high)
        def _():
            rim_copy(1).start()

        for block in (1, 2, 3, 4):
            gather_block(block)

        @pl.when(has_low)
        def _():
            rcopy(rim.at[0], rim.at[0], rim_send.at[0], rim_recv.at[0], core).wait_recv()
            accum[1] = accum[1] + rim[0]

        @pl.when(has_high)
        def _():
            rcopy(rim.at[1], rim.at[1], rim_send.at[1], rim_recv.at[1], core).wait_recv()
            accum[4] = accum[4] + rim[1]

        for half in (0, 1):
            out_copy(half).start()
        for half in (0, 1):
            out_ref[0, :, :, half * HALO : (half + 1) * HALO] = accum[1 + 2 * d + half]
        for half in (0, 1):
            out_copy(half).wait_send()
        to_beside(d, 1).wait_send()
        to_beside(1 - d, 2).wait_send()

        @pl.when(has_low)
        def _():
            rim_copy(0).wait_send()

        @pl.when(has_high)
        def _():
            rim_copy(1).wait_send()

        meas_copy.wait_send()

    @pl.when(not_owner)
    def _():
        to_across().wait_send()
        for half in (0, 1):
            out_copy(half).wait_recv()

    v_copy.wait_send()

    @pl.when(c == m)
    def _():
        probe_copy.wait_send()

    def placed_done(src, block, send, depth):
        @pl.when(d != depth)
        def _():
            rcopy(src, ext_near.at[block], send, ext_sem.at[0, block], across).wait_send()

    placed_done(half_of(0), 1, src_sem.at[0], c)
    placed_done(half_of(1), 2, src_sem.at[1], c)
    placed_done(half_of(1 - c), inner_block, src_sem.at[2], 1 - c)

    @pl.when(has_outer)
    def _():
        outer_copy(0).wait_send()

    for s in (0, 1):
        for i in (0, 1):

            @pl.when(is_owner)
            def _():
                forward_copy(s, i, 1 + i).wait_send()

            @pl.when(jnp.logical_and(not_owner, jnp.logical_not(missing(i))))
            def _():
                forward_copy(s, i, 3 * i).wait_send()


def body(pairs, probe, object_slices, positions, measured):
    n = probe.shape[-1]
    rows = object_slices.shape[2]
    room = rows - n
    f32 = jnp.float32
    tables = jnp.asarray(dft_tables(n))
    transfer = jnp.asarray(propagator(n))
    vmem = pl.BlockSpec(memory_space=pltpu.VMEM)
    anywhere = pl.BlockSpec(memory_space=pl.ANY)
    dma = pltpu.SemaphoreType.DMA
    return pl.pallas_call(
        functools.partial(kernel, pairs),
        out_shape=jax.ShapeDtypeStruct(object_slices.shape, f32),
        in_specs=[vmem, vmem, pl.BlockSpec(memory_space=pltpu.SMEM), vmem, anywhere, anywhere],
        out_specs=vmem,
        scratch_shapes=[
            pltpu.VMEM((5, 2, rows, HALO), f32),
            pltpu.VMEM((5, 2, rows, HALO), f32),
            pltpu.VMEM((2, n, n), f32),
            pltpu.VMEM((2, n, n), f32),
            pltpu.VMEM((2, 2, n, n), f32),
            pltpu.VMEM((n, n), f32),
            pltpu.SMEM(positions.shape, jnp.int32),
            pltpu.VMEM(tables.shape, jnp.bfloat16),
            pltpu.VMEM(transfer.shape, f32),
            pltpu.VMEM((n, n), f32),
            pltpu.VMEM((n, n), f32),
            pltpu.VMEM((2, 2, n, HALO), f32),
            pltpu.VMEM((2, 2, n, HALO), f32),
            pltpu.VMEM((2, 2, 7, 2, n + 2 * room, HALO), f32),
            pltpu.VMEM((6, 2, rows, HALO), f32),
            pltpu.VMEM((2, 2, rows, HALO), f32),
            dma((2,)),
            dma((4,)),
            dma((2, 2)),
            dma((2, 4)),
            dma((2,)),
            dma((3,)),
            dma((3,)),
            dma((2,)),
            dma((2,)),
            dma((3,)),
            dma((3,)),
            dma((2,)),
            dma((2,)),
            dma((2,)),
            dma((2,)),
        ],
        compiler_params=pltpu.CompilerParams(
            collective_id=0, has_side_effects=True, vmem_limit_bytes=60 * 1024 * 1024
        ),
    )(probe, object_slices, positions, measured, tables, transfer)


def solution(mesh):
    placed = (
        P("mode", None, None, None),
        P("depth", None, None, "tile"),
        P("tile", None),
        P("tile", None, None),
    )
    pairs = mesh.shape["tile"] // 2
    return jax.shard_map(
        functools.partial(body, pairs),
        mesh=mesh,
        in_specs=placed,
        out_specs=P("depth", None, None, "tile"),
        check_vma=False,
    )
```

```python
import functools
import math

import jax
import jax.numpy as jnp
import numpy as np
from jax import lax
from jax.experimental import pallas as pl
from jax.experimental.pallas import tpu as pltpu
from jax.sharding import PartitionSpec as P

HALO = 128
MESH = pl.DeviceIdType.MESH


def split_table(table):
    high = table.astype(jnp.bfloat16)
    low = (table - high.astype(np.float64)).astype(jnp.bfloat16)
    return np.stack([high, low], 0)


def dft_tables(length):
    ordinal = np.arange(length)
    angle = 2.0 * math.pi / length * (ordinal[:, None] * ordinal[None, :] % length)
    cosine = np.cos(angle) / math.sqrt(length)
    sine = np.sin(angle) / math.sqrt(length)
    first = np.block([[cosine, -sine], [sine, cosine]])
    second = np.block([[cosine, sine], [-sine, cosine]])
    return np.stack([split_table(first), split_table(second)], 0)


def propagator(length):
    ordinal = np.arange(length)
    signed = np.where(ordinal < length - length // 2, ordinal, ordinal - length)
    square = signed[:, None] * signed[:, None] + signed[None, :] * signed[None, :]
    angle = -math.pi / (2.0 * length) * (3 * square % (4 * length))
    return np.stack([np.cos(angle), np.sin(angle)], 0).astype(np.float32)


def parts_of(value):
    high = value.astype(jnp.bfloat16)
    low = (value - high.astype(jnp.float32)).astype(jnp.bfloat16)
    return high, low


def mm(a, b):
    return jnp.dot(a, b, preferred_element_type=jnp.float32)


def transform(real, imag, tab, right, left):
    n = real.shape[0]
    high, low = parts_of(jnp.concatenate([real, imag], axis=1))
    half = mm(high, tab[right, 0]) + mm(low, tab[right, 0]) + mm(high, tab[right, 1])
    high, low = parts_of(jnp.concatenate([half[:, :n], half[:, n:]], axis=0))
    full = mm(tab[left, 0], high) + mm(tab[left, 0], low) + mm(tab[left, 1], high)
    return full[:n], full[n:]


def kernel(
    pairs,
    probe_ref,
    obj_ref,
    pos_ref,
    meas_ref,
    tab_hbm,
    prop_hbm,
    out_ref,
    ext_near,
    ext_far,
    psi0,
    psi1,
    win,
    pattern,
    posn,
    tab,
    prop,
    mine_int,
    their_int,
    vsend,
    vrecv,
    spread_r,
    spread_i,
    accum,
    rim,
    load_sem,
    src_sem,
    fwd_sem,
    ext_sem,
    pos_sem,
    probe_sem,
    meas_sem,
    int_sem,
    v_sem,
    w_send,
    w_recv,
    rim_send,
    rim_recv,
    out_send,
    out_recv,
):
    n = psi0.shape[1]
    rows = obj_ref.shape[2]
    room = rows - n
    d = lax.axis_index("depth")
    m = lax.axis_index("mode")
    t = lax.axis_index("tile")
    c = lax.rem(t, 2)
    z = t // 2
    other = t + 1 - 2 * c
    own = 1 - (c - d) * (c - d)
    core = {"tile": other}
    across = {"depth": 1 - d}
    beside = {"mode": 1 - m}
    is_owner = c == d
    not_owner = c != d

    def rcopy(src, dst, send, recv, target):
        return pltpu.make_async_remote_copy(
            src_ref=src, dst_ref=dst, send_sem=send, recv_sem=recv, device_id=target, device_id_type=MESH
        )

    loads = [
        pltpu.make_async_copy(tab_hbm, tab, load_sem.at[0]),
        pltpu.make_async_copy(prop_hbm, prop, load_sem.at[1]),
    ]
    for item in loads:
        item.start()

    barrier = pltpu.get_barrier_semaphore()
    for target in (core, across, beside):
        pl.semaphore_signal(barrier, inc=1, device_id=target, device_id_type=MESH)

    @pl.when(z > 0)
    def _():
        for depth in (0, 1):
            pl.semaphore_signal(barrier, inc=1, device_id={"depth": depth, "tile": t - 2}, device_id_type=MESH)

    @pl.when(z < pairs - 1)
    def _():
        for depth in (0, 1):
            pl.semaphore_signal(barrier, inc=1, device_id={"depth": depth, "tile": t + 2}, device_id_type=MESH)

    peers = 3 + 2 * jnp.minimum(z, 1) + 2 * jnp.minimum(pairs - 1 - z, 1)
    pl.semaphore_wait(barrier, peers)

    ext = (ext_near, ext_far)
    spread = (spread_r, spread_i)

    def half_of(h):
        return obj_ref.at[0, :, :, pl.ds(pl.multiple_of(h * HALO, HALO), HALO)]

    def place(src, block, send, depth):
        for s in (0, 1):
            dst = ext[s].at[block]
            sem = ext_sem.at[s, block]

            @pl.when(jnp.logical_and(d == s, depth == s))
            def _():
                pltpu.make_async_copy(src, dst, sem).start()

            @pl.when(jnp.logical_and(d == s, depth != s))
            def _():
                rcopy(src, dst, send, sem, across).start()

    inner_block = 3 * c
    outer_block = 3 - 3 * c
    outer_tile = t - 2 + 4 * c
    has_outer = jnp.logical_or(jnp.logical_and(c == 0, z > 0), jnp.logical_and(c == 1, z < pairs - 1))

    def outer_copy(s):
        return rcopy(
            half_of(c),
            ext[s].at[outer_block],
            src_sem.at[3],
            ext_sem.at[s, outer_block],
            {"depth": 1 - c, "tile": outer_tile},
        )

    pos_copy = rcopy(pos_ref, posn, pos_sem.at[0], pos_sem.at[1], core)
    pos_copy.start()
    place(half_of(0), 1, src_sem.at[0], c)
    place(half_of(1), 2, src_sem.at[1], c)
    place(half_of(1 - c), inner_block, src_sem.at[2], 1 - c)

    for s in (0, 1):

        @pl.when(jnp.logical_and(has_outer, d == s))
        def _():
            outer_copy(s).start()

    probe_copy = rcopy(probe_ref.at[0], psi0, probe_sem.at[0], probe_sem.at[1], beside)

    @pl.when(c == m)
    def _():
        probe_copy.start()
        pltpu.make_async_copy(probe_ref.at[0], psi0, probe_sem.at[2]).start()

    meas_copy = rcopy(meas_ref.at[m], pattern, meas_sem.at[0], meas_sem.at[1], core)
    meas_local = pltpu.make_async_copy(meas_ref.at[m], pattern, meas_sem.at[2])

    @pl.when(is_owner)
    def _():
        meas_copy.start()
        meas_local.start()

    for s in (0, 1):
        ext[s][4] = jnp.zeros(ext_near.shape[1:], jnp.float32)

    no_left = jnp.logical_and(d == 0, z == 0)
    no_right = jnp.logical_and(d == 1, z == pairs - 1)

    @pl.when(no_left)
    def _():
        for s in (0, 1):
            ext[s][0] = jnp.zeros(ext_near.shape[1:], jnp.float32)

    @pl.when(no_right)
    def _():
        for s in (0, 1):
            ext[s][3] = jnp.zeros(ext_near.shape[1:], jnp.float32)

    @pl.when(is_owner)
    def _():
        @pl.loop(0, 4)
        def _(w):
            for field in spread:
                for j in (0, 1, 2, 5, 6):
                    field[w // 2, lax.rem(w, 2), j] = jnp.zeros(field.shape[3:], jnp.float32)
                for j in (3, 4):
                    for edge in (0, room + n):
                        field[w // 2, lax.rem(w, 2), j, edge : edge + room, :] = jnp.zeros((room, HALO), jnp.float32)

    def ext_wait(s, block):
        rcopy(ext[s].at[block], ext[s].at[block], src_sem.at[0], ext_sem.at[s, block], core).wait_recv()

    def forward_copy(s, i, block):
        return rcopy(ext[s].at[block], ext[s].at[block], fwd_sem.at[s, i], ext_sem.at[s, block], core)

    def missing(i):
        return no_left if i == 0 else no_right

    def land(s):
        for i in (0, 1):

            @pl.when(is_owner)
            def _():
                ext_wait(s, 1 + i)
                forward_copy(s, i, 1 + i).start()

            @pl.when(jnp.logical_and(not_owner, jnp.logical_not(missing(i))))
            def _():
                ext_wait(s, 3 * i)
                forward_copy(s, i, 3 * i).start()

    def arrive(s):
        for i in (0, 1):

            @pl.when(not_owner)
            def _():
                ext_wait(s, 1 + i)

            @pl.when(jnp.logical_and(is_owner, jnp.logical_not(missing(i))))
            def _():
                ext_wait(s, 3 * i)

    lane = lax.broadcasted_iota(jnp.int32, (1, HALO), 1)

    def place_of(tile_no, which):
        mine = tile_no == c
        top = jnp.where(mine, pos_ref[which, 0], posn[which, 0])
        left = jnp.where(mine, pos_ref[which, 1], posn[which, 1])
        return top, left // HALO, lax.rem(left, HALO)

    def cut(s, spot):
        top, block, rem = spot
        back = lax.rem(HALO - rem, HALO)
        for part in (0, 1):
            for j in (0, 1):
                near = ext[s][block + j, part, pl.ds(top, n), :]
                far = ext[s][block + j + 1, part, pl.ds(top, n), :]
                mixed = jnp.where(lane >= rem, near, far)
                win[s, part, :, j * HALO : (j + 1) * HALO] = pltpu.roll(mixed, back, 1)

    @pl.when(d == 1)
    def _():
        land(1)

    land(0)
    for item in loads:
        item.wait()
    pos_copy.wait()

    @pl.when(c == m)
    def _():
        pltpu.make_async_copy(probe_ref.at[0], psi0, probe_sem.at[2]).wait()

    @pl.when(c != m)
    def _():
        probe_copy.wait_recv()

    spot = place_of(d, m)
    arrive(0)
    cut(0, spot)
    wr, wi = win[0, 0], win[0, 1]
    pr, pi = psi0[0], psi0[1]
    spec_r, spec_i = transform(pr * wr - pi * wi, pr * wi + pi * wr, tab, 0, 1)
    hr, hi = prop[0], prop[1]
    wave_r, wave_i = transform(spec_r * hr - spec_i * hi, spec_r * hi + spec_i * hr, tab, 1, 0)
    psi1[0] = wave_r
    psi1[1] = wave_i

    @pl.when(d == 0)
    def _():
        land(1)

    arrive(1)
    cut(1, spot)
    wr, wi = win[1, 0], win[1, 1]
    wave_r, wave_i = psi1[0], psi1[1]
    far_r, far_i = transform(wave_r * wr - wave_i * wi, wave_r * wi + wave_i * wr, tab, 0, 1)
    mine_int[...] = far_r * far_r + far_i * far_i
    int_copy = rcopy(mine_int, their_int, int_sem.at[0], int_sem.at[1], core)
    int_copy.start()

    @pl.when(is_owner)
    def _():
        meas_local.wait()

    @pl.when(not_owner)
    def _():
        meas_copy.wait_recv()

    int_copy.wait()
    resid = mine_int[...] + their_int[...] - pattern[...]
    q_r, q_i = transform(resid * far_r, resid * far_i, tab, 1, 0)

    def v_copy(part):
        return rcopy(vsend.at[part], vrecv.at[part], v_sem.at[0, part], v_sem.at[1, part], core)

    def window_at(tile_no, which, part):
        return spread[part].at[tile_no, which, 3:5, room : room + n, :]

    def give(real, imag):
        for part, value in enumerate((real, imag)):
            for j in (0, 1):
                vsend[part, j] = value[:, j * HALO : (j + 1) * HALO]
            v_copy(part).start()

    def keep(real, imag):
        for part, value in enumerate((real, imag)):
            for j in (0, 1):
                spread[part][d, m, 3 + j, room : room + n, :] = value[:, j * HALO : (j + 1) * HALO]

    def carry(tile_no, which, part, k, j, target):
        ref = window_at(tile_no, which, part)
        return rcopy(ref, ref, w_send.at[k, part], w_recv.at[j, part], target)

    def to_across(part):
        return carry(d, m, part, 0, 0, across)

    def to_beside(part):
        return carry(d, m, part, 1, 1, beside)

    def aside():
        return carry(d, m, 1, 1, 3, beside)

    def relay_beside():
        return carry(1 - d, m, 0, 2, 2, beside)

    def relay_across():
        return carry(d, 1 - m, 1, 2, 2, across)

    def finish():
        for part in (0, 1):
            v_copy(part).wait_recv()
            here = window_at(d, m, part)
            here[...] = here[...] + vrecv[part]

            @pl.when(is_owner)
            def _():
                to_beside(part).start()

            @pl.when(not_owner)
            def _():
                if part == 1:
                    aside().start()
                to_across(part).start()

    wr, wi = win[1, 0], win[1, 1]
    wave_r, wave_i = psi1[0], psi1[1]
    v_r = wave_r * q_r + wave_i * q_i
    v_i = wave_r * q_i - wave_i * q_r

    @pl.when(c == 0)
    def _():
        give(v_r, v_i)

    @pl.when(c == 1)
    def _():
        keep(v_r, v_i)

    spec_r, spec_i = transform(wr * q_r + wi * q_i, wr * q_i - wi * q_r, tab, 0, 1)

    @pl.when(c == 1)
    def _():
        finish()

    hr, hi = prop[0], prop[1]
    q_r, q_i = transform(spec_r * hr + spec_i * hi, spec_i * hr - spec_r * hi, tab, 1, 0)
    pr, pi = psi0[0], psi0[1]
    v_r = pr * q_r + pi * q_i
    v_i = pr * q_i - pi * q_r

    @pl.when(c == 1)
    def _():
        give(v_r, v_i)

    @pl.when(c == 0)
    def _():
        keep(v_r, v_i)
        finish()

    def placed(tile_no, which, block, part):
        top, first, rem = place_of(tile_no, which)
        at = block - first + 3
        near = spread[part][tile_no, which, at, pl.ds(room - top, rows), :]
        far = spread[part][tile_no, which, at - 1, pl.ds(room - top, rows), :]
        return pltpu.roll(jnp.where(lane < HALO - rem, near, far), rem, 1)

    def gather_block(block, part):
        terms = []
        for tile_no in (0, 1):
            local = block - 2 * tile_no
            if 0 <= local < 4:
                for which in (0, 1):
                    terms.append(placed(tile_no, which, local, part))
        accum[block, part] = functools.reduce(jnp.add, terms)

    def rim_copy(side, part):
        return rcopy(
            accum.at[5 * side, part],
            rim.at[1 - side, part],
            rim_send.at[side, part],
            rim_recv.at[1 - side, part],
            {"tile": t - 2 + 4 * side},
        )

    def out_copy(outer, part):
        half = d * (1 - outer) + (1 - d) * outer
        block = 3 - 2 * d + half
        return rcopy(
            accum.at[block, part],
            out_ref.at[0, part, :, pl.ds(pl.multiple_of(half * HALO, HALO), HALO)],
            out_send.at[outer, part],
            out_recv.at[outer, part],
            core,
        )

    has_low = z > 0
    has_high = z < pairs - 1

    @pl.when(is_owner)
    def _():
        carry(1 - d, m, 0, 2, 0, across).wait_recv()
        relay_beside().start()
        for part in (0, 1):
            if part == 1:
                carry(1 - d, m, 1, 2, 0, across).wait_recv()
            carry(d, 1 - m, part, 2, 1, beside).wait_recv()
            carry(1 - d, 1 - m, part, 2, 2, beside).wait_recv()
            gather_block(0, part)

            @pl.when(has_low)
            def _():
                rim_copy(0, part).start()

            gather_block(5, part)

            @pl.when(has_high)
            def _():
                rim_copy(1, part).start()

            for block in (2, 3):
                gather_block(block, part)
            out_copy(0, part).start()
            for block in (1, 4):
                gather_block(block, part)
        for part in (0, 1):
            for side, block, there in ((0, 1, has_low), (1, 4, has_high)):

                @pl.when(there)
                def _():
                    rcopy(
                        rim.at[side, part], rim.at[side, part], rim_send.at[side, part], rim_recv.at[side, part], core
                    ).wait_recv()
                    accum[block, part] = accum[block, part] + rim[side, part]

            out_copy(1, part).start()
            for half in (0, 1):
                out_ref[0, part, :, half * HALO : (half + 1) * HALO] = accum[1 + 2 * d + half, part]
        relay_beside().wait_send()
        for part in (0, 1):
            to_beside(part).wait_send()
            for outer in (0, 1):
                out_copy(outer, part).wait_send()
            for side, there in ((0, has_low), (1, has_high)):

                @pl.when(there)
                def _():
                    rim_copy(side, part).wait_send()

        meas_copy.wait_send()

    @pl.when(not_owner)
    def _():
        carry(d, 1 - m, 1, 2, 3, beside).wait_recv()
        relay_across().start()
        for part in (0, 1):
            to_across(part).wait_send()
        aside().wait_send()
        relay_across().wait_send()
        for part in (0, 1):
            for outer in (0, 1):
                out_copy(outer, part).wait_recv()

    for part in (0, 1):
        v_copy(part).wait_send()

    @pl.when(c == m)
    def _():
        probe_copy.wait_send()

    def placed_done(src, block, send, depth):
        @pl.when(d != depth)
        def _():
            rcopy(src, ext_near.at[block], send, ext_sem.at[0, block], across).wait_send()

    placed_done(half_of(0), 1, src_sem.at[0], c)
    placed_done(half_of(1), 2, src_sem.at[1], c)
    placed_done(half_of(1 - c), inner_block, src_sem.at[2], 1 - c)

    @pl.when(has_outer)
    def _():
        outer_copy(0).wait_send()

    for s in (0, 1):
        for i in (0, 1):

            @pl.when(is_owner)
            def _():
                forward_copy(s, i, 1 + i).wait_send()

            @pl.when(jnp.logical_and(not_owner, jnp.logical_not(missing(i))))
            def _():
                forward_copy(s, i, 3 * i).wait_send()


def body(pairs, probe, object_slices, positions, measured):
    n = probe.shape[-1]
    rows = object_slices.shape[2]
    room = rows - n
    f32 = jnp.float32
    tables = jnp.asarray(dft_tables(n))
    transfer = jnp.asarray(propagator(n))
    vmem = pl.BlockSpec(memory_space=pltpu.VMEM)
    anywhere = pl.BlockSpec(memory_space=pl.ANY)
    dma = pltpu.SemaphoreType.DMA
    return pl.pallas_call(
        functools.partial(kernel, pairs),
        out_shape=jax.ShapeDtypeStruct(object_slices.shape, f32),
        in_specs=[vmem, vmem, pl.BlockSpec(memory_space=pltpu.SMEM), vmem, anywhere, anywhere],
        out_specs=vmem,
        scratch_shapes=[
            pltpu.VMEM((5, 2, rows, HALO), f32),
            pltpu.VMEM((5, 2, rows, HALO), f32),
            pltpu.VMEM((2, n, n), f32),
            pltpu.VMEM((2, n, n), f32),
            pltpu.VMEM((2, 2, n, n), f32),
            pltpu.VMEM((n, n), f32),
            pltpu.SMEM(positions.shape, jnp.int32),
            pltpu.VMEM(tables.shape, jnp.bfloat16),
            pltpu.VMEM(transfer.shape, f32),
            pltpu.VMEM((n, n), f32),
            pltpu.VMEM((n, n), f32),
            pltpu.VMEM((2, 2, n, HALO), f32),
            pltpu.VMEM((2, 2, n, HALO), f32),
            pltpu.VMEM((2, 2, 7, n + 2 * room, HALO), f32),
            pltpu.VMEM((2, 2, 7, n + 2 * room, HALO), f32),
            pltpu.VMEM((6, 2, rows, HALO), f32),
            pltpu.VMEM((2, 2, rows, HALO), f32),
            dma((2,)),
            dma((4,)),
            dma((2, 2)),
            dma((2, 4)),
            dma((2,)),
            dma((3,)),
            dma((3,)),
            dma((2,)),
            dma((2, 2)),
            dma((3, 2)),
            dma((4, 2)),
            dma((2, 2)),
            dma((2, 2)),
            dma((2, 2)),
            dma((2, 2)),
        ],
        compiler_params=pltpu.CompilerParams(
            collective_id=0, has_side_effects=True, vmem_limit_bytes=60 * 1024 * 1024
        ),
    )(probe, object_slices, positions, measured, tables, transfer)


def solution(mesh):
    placed = (
        P("mode", None, None, None),
        P("depth", None, None, "tile"),
        P("tile", None),
        P("tile", None, None),
    )
    pairs = mesh.shape["tile"] // 2
    return jax.shard_map(
        functools.partial(body, pairs),
        mesh=mesh,
        in_specs=placed,
        out_specs=P("depth", None, None, "tile"),
        check_vma=False,
    )
```

```python
import functools
import math

import jax
import jax.numpy as jnp
import numpy as np
from jax import lax
from jax.experimental import pallas as pl
from jax.experimental.pallas import tpu as pltpu
from jax.sharding import PartitionSpec as P

HALO = 128
MESH = pl.DeviceIdType.MESH


def split_table(table):
    high = table.astype(jnp.bfloat16)
    low = (table - high.astype(np.float64)).astype(jnp.bfloat16)
    return np.stack([high, low], 0)


def dft_tables(length):
    ordinal = np.arange(length)
    angle = 2.0 * math.pi / length * (ordinal[:, None] * ordinal[None, :] % length)
    cosine = np.cos(angle) / math.sqrt(length)
    sine = np.sin(angle) / math.sqrt(length)
    first = np.block([[cosine, -sine], [sine, cosine]])
    second = np.block([[cosine, sine], [-sine, cosine]])
    return np.stack([split_table(first), split_table(second)], 0)


def propagator(length):
    ordinal = np.arange(length)
    signed = np.where(ordinal < length - length // 2, ordinal, ordinal - length)
    square = signed[:, None] * signed[:, None] + signed[None, :] * signed[None, :]
    angle = -math.pi / (2.0 * length) * (3 * square % (4 * length))
    return np.stack([np.cos(angle), np.sin(angle)], 0).astype(np.float32)


def parts_of(value):
    high = value.astype(jnp.bfloat16)
    low = (value - high.astype(jnp.float32)).astype(jnp.bfloat16)
    return high, low


def mm(a, b):
    return jnp.dot(a, b, preferred_element_type=jnp.float32)


def transform(real, imag, tab, right, left):
    n = real.shape[0]
    high, low = parts_of(jnp.concatenate([real, imag], axis=1))
    half = mm(high, tab[right, 0]) + mm(low, tab[right, 0]) + mm(high, tab[right, 1])
    high, low = parts_of(jnp.concatenate([half[:, :n], half[:, n:]], axis=0))
    full = mm(tab[left, 0], high) + mm(tab[left, 0], low) + mm(tab[left, 1], high)
    return full[:n], full[n:]


def kernel(
    pairs,
    probe_ref,
    obj_ref,
    pos_ref,
    meas_ref,
    tab_hbm,
    prop_hbm,
    out_ref,
    ext_near,
    ext_far,
    psi0,
    psi1,
    win,
    pattern,
    posn,
    tab,
    prop,
    mine_int,
    their_int,
    vsend,
    vrecv,
    spread_r,
    spread_i,
    accum,
    rim,
    load_sem,
    src_sem,
    fwd_sem,
    relay_sem,
    ext_sem,
    pos_sem,
    probe_sem,
    meas_sem,
    int_sem,
    v_sem,
    w_send,
    w_recv,
    rim_send,
    rim_recv,
    out_send,
    out_recv,
):
    n = psi0.shape[1]
    rows = obj_ref.shape[2]
    room = rows - n
    d = lax.axis_index("depth")
    m = lax.axis_index("mode")
    t = lax.axis_index("tile")
    c = lax.rem(t, 2)
    z = t // 2
    other = t + 1 - 2 * c
    own = 1 - (c - d) * (c - d)
    core = {"tile": other}
    across = {"depth": 1 - d}
    beside = {"mode": 1 - m}
    is_owner = c == d
    not_owner = c != d

    def rcopy(src, dst, send, recv, target):
        return pltpu.make_async_remote_copy(
            src_ref=src, dst_ref=dst, send_sem=send, recv_sem=recv, device_id=target, device_id_type=MESH
        )

    loads = [
        pltpu.make_async_copy(tab_hbm, tab, load_sem.at[0]),
        pltpu.make_async_copy(prop_hbm, prop, load_sem.at[1]),
    ]
    for item in loads:
        item.start()

    barrier = pltpu.get_barrier_semaphore()
    for target in (core, across, beside):
        pl.semaphore_signal(barrier, inc=1, device_id=target, device_id_type=MESH)

    @pl.when(z > 0)
    def _():
        for depth in (0, 1):
            pl.semaphore_signal(barrier, inc=1, device_id={"depth": depth, "tile": t - 2}, device_id_type=MESH)

    @pl.when(z < pairs - 1)
    def _():
        for depth in (0, 1):
            pl.semaphore_signal(barrier, inc=1, device_id={"depth": depth, "tile": t + 2}, device_id_type=MESH)

    peers = 3 + 2 * jnp.minimum(z, 1) + 2 * jnp.minimum(pairs - 1 - z, 1)
    pl.semaphore_wait(barrier, peers)

    ext = (ext_near, ext_far)
    spread = (spread_r, spread_i)

    tall = rows // 2

    def strip(r):
        return pl.ds(pl.multiple_of(r * tall, 8), tall)

    def half_of(h, r):
        return obj_ref.at[0, :, strip(r), pl.ds(pl.multiple_of(h * HALO, HALO), HALO)]

    def slot(s, block, r):
        return ext[s].at[block, :, strip(r), :]

    def place(h, block, send, depth):
        for s in (0, 1):

            @pl.when(jnp.logical_and(d == s, depth == s))
            def _():
                for r in (0, 1):
                    pltpu.make_async_copy(half_of(h, r), slot(s, block, r), ext_sem.at[s, block, r]).start()

            @pl.when(jnp.logical_and(d == s, depth != s))
            def _():
                rcopy(half_of(h, m), slot(s, block, m), send, ext_sem.at[s, block, m], across).start()

    inner_block = 3 * c
    outer_block = 3 - 3 * c
    outer_tile = t - 2 + 4 * c
    has_outer = jnp.logical_or(jnp.logical_and(c == 0, z > 0), jnp.logical_and(c == 1, z < pairs - 1))

    def outer_copy(s, r):
        return rcopy(
            half_of(c, r),
            slot(s, outer_block, r),
            src_sem.at[3 + r],
            ext_sem.at[s, outer_block, r],
            {"depth": 1 - c, "tile": outer_tile},
        )

    pos_copy = rcopy(pos_ref, posn, pos_sem.at[0], pos_sem.at[1], core)
    pos_copy.start()
    place(0, 1, src_sem.at[0], c)
    place(1, 2, src_sem.at[1], c)
    place(1 - c, inner_block, src_sem.at[2], 1 - c)

    for s in (0, 1):

        @pl.when(jnp.logical_and(has_outer, d == s))
        def _():
            for r in (0, 1):
                outer_copy(s, r).start()

    probe_copy = rcopy(probe_ref.at[0], psi0, probe_sem.at[0], probe_sem.at[1], beside)

    @pl.when(c == m)
    def _():
        probe_copy.start()
        pltpu.make_async_copy(probe_ref.at[0], psi0, probe_sem.at[2]).start()

    meas_copy = rcopy(meas_ref.at[m], pattern, meas_sem.at[0], meas_sem.at[1], core)
    meas_local = pltpu.make_async_copy(meas_ref.at[m], pattern, meas_sem.at[2])

    @pl.when(is_owner)
    def _():
        meas_copy.start()
        meas_local.start()

    for s in (0, 1):
        ext[s][4] = jnp.zeros(ext_near.shape[1:], jnp.float32)

    no_left = jnp.logical_and(d == 0, z == 0)
    no_right = jnp.logical_and(d == 1, z == pairs - 1)

    @pl.when(no_left)
    def _():
        for s in (0, 1):
            ext[s][0] = jnp.zeros(ext_near.shape[1:], jnp.float32)

    @pl.when(no_right)
    def _():
        for s in (0, 1):
            ext[s][3] = jnp.zeros(ext_near.shape[1:], jnp.float32)

    @pl.when(is_owner)
    def _():
        @pl.loop(0, 4)
        def _(w):
            for field in spread:
                for j in (0, 1, 2, 5, 6):
                    field[w // 2, lax.rem(w, 2), j] = jnp.zeros(field.shape[3:], jnp.float32)
                for j in (3, 4):
                    for edge in (0, room + n):
                        field[w // 2, lax.rem(w, 2), j, edge : edge + room, :] = jnp.zeros((room, HALO), jnp.float32)

    def ext_wait(s, block, r):
        ref = slot(s, block, r)
        rcopy(ref, ref, src_sem.at[0], ext_sem.at[s, block, r], core).wait_recv()

    def forward_copy(s, i, block, r):
        ref = slot(s, block, r)
        return rcopy(ref, ref, fwd_sem.at[s, i, r], ext_sem.at[s, block, r], core)

    def relay_copy(s, i, block):
        ref = slot(s, block, m)
        return rcopy(ref, ref, relay_sem.at[s, i], ext_sem.at[s, block, m], beside)

    def missing(i):
        return no_left if i == 0 else no_right

    def lands(i):
        return jnp.logical_and(not_owner, jnp.logical_not(missing(i)))

    def relays(s, i):
        return jnp.logical_and(d != s, jnp.logical_and(not_owner, d != i))

    def land(s, second):
        r = 1 - m if second else m
        for i in (0, 1):

            @pl.when(is_owner)
            def _():
                ext_wait(s, 1 + i, r)
                forward_copy(s, i, 1 + i, r).start()

            @pl.when(lands(i))
            def _():
                ext_wait(s, 3 * i, r)
                forward_copy(s, i, 3 * i, r).start()

            if not second:

                @pl.when(jnp.logical_and(is_owner, d != s))
                def _():
                    relay_copy(s, i, 1 + i).start()

                @pl.when(relays(s, i))
                def _():
                    relay_copy(s, i, 3 * i).start()

    def arrive(s):
        for i in (0, 1):
            for r in (0, 1):

                @pl.when(not_owner)
                def _():
                    ext_wait(s, 1 + i, r)

                @pl.when(jnp.logical_and(is_owner, jnp.logical_not(missing(i))))
                def _():
                    ext_wait(s, 3 * i, r)

    lane = lax.broadcasted_iota(jnp.int32, (1, HALO), 1)

    def place_of(tile_no, which):
        mine = tile_no == c
        top = jnp.where(mine, pos_ref[which, 0], posn[which, 0])
        left = jnp.where(mine, pos_ref[which, 1], posn[which, 1])
        return top, left // HALO, lax.rem(left, HALO)

    def cut(s, spot):
        top, block, rem = spot
        back = lax.rem(HALO - rem, HALO)
        for part in (0, 1):
            for j in (0, 1):
                near = ext[s][block + j, part, pl.ds(top, n), :]
                far = ext[s][block + j + 1, part, pl.ds(top, n), :]
                mixed = jnp.where(lane >= rem, near, far)
                win[s, part, :, j * HALO : (j + 1) * HALO] = pltpu.roll(mixed, back, 1)

    @pl.when(d == 1)
    def _():
        land(1, False)
        land(1, True)

    land(0, False)
    land(0, True)

    @pl.when(d == 0)
    def _():
        land(1, False)

    for item in loads:
        item.wait()
    pos_copy.wait()

    @pl.when(c == m)
    def _():
        pltpu.make_async_copy(probe_ref.at[0], psi0, probe_sem.at[2]).wait()

    @pl.when(c != m)
    def _():
        probe_copy.wait_recv()

    spot = place_of(d, m)
    arrive(0)
    cut(0, spot)
    wr, wi = win[0, 0], win[0, 1]
    pr, pi = psi0[0], psi0[1]
    spec_r, spec_i = transform(pr * wr - pi * wi, pr * wi + pi * wr, tab, 0, 1)
    hr, hi = prop[0], prop[1]
    wave_r, wave_i = transform(spec_r * hr - spec_i * hi, spec_r * hi + spec_i * hr, tab, 1, 0)
    psi1[0] = wave_r
    psi1[1] = wave_i

    @pl.when(d == 0)
    def _():
        land(1, True)

    arrive(1)
    cut(1, spot)
    wr, wi = win[1, 0], win[1, 1]
    wave_r, wave_i = psi1[0], psi1[1]
    far_r, far_i = transform(wave_r * wr - wave_i * wi, wave_r * wi + wave_i * wr, tab, 0, 1)
    mine_int[...] = far_r * far_r + far_i * far_i
    int_copy = rcopy(mine_int, their_int, int_sem.at[0], int_sem.at[1], core)
    int_copy.start()

    @pl.when(is_owner)
    def _():
        meas_local.wait()

    @pl.when(not_owner)
    def _():
        meas_copy.wait_recv()

    int_copy.wait()
    resid = mine_int[...] + their_int[...] - pattern[...]
    q_r, q_i = transform(resid * far_r, resid * far_i, tab, 1, 0)

    def v_copy(part):
        return rcopy(vsend.at[part], vrecv.at[part], v_sem.at[0, part], v_sem.at[1, part], core)

    def window_at(tile_no, which, part):
        return spread[part].at[tile_no, which, 3:5, room : room + n, :]

    def give(real, imag):
        for part, value in enumerate((real, imag)):
            for j in (0, 1):
                vsend[part, j] = value[:, j * HALO : (j + 1) * HALO]
            v_copy(part).start()

    def keep(real, imag):
        for part, value in enumerate((real, imag)):
            for j in (0, 1):
                spread[part][d, m, 3 + j, room : room + n, :] = value[:, j * HALO : (j + 1) * HALO]

    def carry(tile_no, which, part, k, j, target):
        ref = window_at(tile_no, which, part)
        return rcopy(ref, ref, w_send.at[k, part], w_recv.at[j, part], target)

    def to_across(part):
        return carry(d, m, part, 0, 0, across)

    def to_beside(part):
        return carry(d, m, part, 1, 1, beside)

    def aside():
        return carry(d, m, 1, 1, 3, beside)

    def relay_beside():
        return carry(1 - d, m, 0, 2, 2, beside)

    def relay_across():
        return carry(d, 1 - m, 1, 2, 2, across)

    def finish():
        for part in (0, 1):
            v_copy(part).wait_recv()
            here = window_at(d, m, part)
            here[...] = here[...] + vrecv[part]

            @pl.when(is_owner)
            def _():
                to_beside(part).start()

            @pl.when(not_owner)
            def _():
                if part == 1:
                    aside().start()
                to_across(part).start()

    wr, wi = win[1, 0], win[1, 1]
    wave_r, wave_i = psi1[0], psi1[1]
    v_r = wave_r * q_r + wave_i * q_i
    v_i = wave_r * q_i - wave_i * q_r

    @pl.when(c == 0)
    def _():
        give(v_r, v_i)

    @pl.when(c == 1)
    def _():
        keep(v_r, v_i)

    spec_r, spec_i = transform(wr * q_r + wi * q_i, wr * q_i - wi * q_r, tab, 0, 1)

    @pl.when(c == 1)
    def _():
        finish()

    hr, hi = prop[0], prop[1]
    q_r, q_i = transform(spec_r * hr + spec_i * hi, spec_i * hr - spec_r * hi, tab, 1, 0)
    pr, pi = psi0[0], psi0[1]
    v_r = pr * q_r + pi * q_i
    v_i = pr * q_i - pi * q_r

    @pl.when(c == 1)
    def _():
        give(v_r, v_i)

    @pl.when(c == 0)
    def _():
        keep(v_r, v_i)
        finish()

    def placed(tile_no, which, block, part):
        top, first, rem = place_of(tile_no, which)
        at = block - first + 3
        near = spread[part][tile_no, which, at, pl.ds(room - top, rows), :]
        far = spread[part][tile_no, which, at - 1, pl.ds(room - top, rows), :]
        return pltpu.roll(jnp.where(lane < HALO - rem, near, far), rem, 1)

    def gather_block(block, part):
        terms = []
        for tile_no in (0, 1):
            local = block - 2 * tile_no
            if 0 <= local < 4:
                for which in (0, 1):
                    terms.append(placed(tile_no, which, local, part))
        accum[block, part] = functools.reduce(jnp.add, terms)

    def rim_copy(side, part):
        return rcopy(
            accum.at[5 * side, part],
            rim.at[1 - side, part],
            rim_send.at[side, part],
            rim_recv.at[1 - side, part],
            {"tile": t - 2 + 4 * side},
        )

    def out_copy(outer, part):
        half = d * (1 - outer) + (1 - d) * outer
        block = 3 - 2 * d + half
        return rcopy(
            accum.at[block, part],
            out_ref.at[0, part, :, pl.ds(pl.multiple_of(half * HALO, HALO), HALO)],
            out_send.at[outer, part],
            out_recv.at[outer, part],
            core,
        )

    has_low = z > 0
    has_high = z < pairs - 1

    @pl.when(is_owner)
    def _():
        carry(1 - d, m, 0, 2, 0, across).wait_recv()
        relay_beside().start()
        for part in (0, 1):
            if part == 1:
                carry(1 - d, m, 1, 2, 0, across).wait_recv()
            carry(d, 1 - m, part, 2, 1, beside).wait_recv()
            carry(1 - d, 1 - m, part, 2, 2, beside).wait_recv()
            gather_block(0, part)

            @pl.when(has_low)
            def _():
                rim_copy(0, part).start()

            gather_block(5, part)

            @pl.when(has_high)
            def _():
                rim_copy(1, part).start()

            for block in (2, 3):
                gather_block(block, part)
            out_copy(0, part).start()
            for block in (1, 4):
                gather_block(block, part)
        for part in (0, 1):
            for side, block, there in ((0, 1, has_low), (1, 4, has_high)):

                @pl.when(there)
                def _():
                    rcopy(
                        rim.at[side, part], rim.at[side, part], rim_send.at[side, part], rim_recv.at[side, part], core
                    ).wait_recv()
                    accum[block, part] = accum[block, part] + rim[side, part]

            out_copy(1, part).start()
            for half in (0, 1):
                out_ref[0, part, :, half * HALO : (half + 1) * HALO] = accum[1 + 2 * d + half, part]
        relay_beside().wait_send()
        for part in (0, 1):
            to_beside(part).wait_send()
            for outer in (0, 1):
                out_copy(outer, part).wait_send()
            for side, there in ((0, has_low), (1, has_high)):

                @pl.when(there)
                def _():
                    rim_copy(side, part).wait_send()

        meas_copy.wait_send()

    @pl.when(not_owner)
    def _():
        carry(d, 1 - m, 1, 2, 3, beside).wait_recv()
        relay_across().start()
        for part in (0, 1):
            to_across(part).wait_send()
        aside().wait_send()
        relay_across().wait_send()
        for part in (0, 1):
            for outer in (0, 1):
                out_copy(outer, part).wait_recv()

    for part in (0, 1):
        v_copy(part).wait_send()

    @pl.when(c == m)
    def _():
        probe_copy.wait_send()

    def placed_done(h, block, send, depth):
        @pl.when(d != depth)
        def _():
            rcopy(half_of(h, m), slot(0, block, m), send, ext_sem.at[0, block, m], across).wait_send()

    placed_done(0, 1, src_sem.at[0], c)
    placed_done(1, 2, src_sem.at[1], c)
    placed_done(1 - c, inner_block, src_sem.at[2], 1 - c)

    @pl.when(has_outer)
    def _():
        for r in (0, 1):
            outer_copy(0, r).wait_send()

    for s in (0, 1):
        for i in (0, 1):

            @pl.when(is_owner)
            def _():
                for r in (0, 1):
                    forward_copy(s, i, 1 + i, r).wait_send()

            @pl.when(lands(i))
            def _():
                for r in (0, 1):
                    forward_copy(s, i, 3 * i, r).wait_send()

            @pl.when(jnp.logical_and(is_owner, d != s))
            def _():
                relay_copy(s, i, 1 + i).wait_send()

            @pl.when(relays(s, i))
            def _():
                relay_copy(s, i, 3 * i).wait_send()


def body(pairs, probe, object_slices, positions, measured):
    n = probe.shape[-1]
    rows = object_slices.shape[2]
    room = rows - n
    f32 = jnp.float32
    tables = jnp.asarray(dft_tables(n))
    transfer = jnp.asarray(propagator(n))
    vmem = pl.BlockSpec(memory_space=pltpu.VMEM)
    anywhere = pl.BlockSpec(memory_space=pl.ANY)
    dma = pltpu.SemaphoreType.DMA
    return pl.pallas_call(
        functools.partial(kernel, pairs),
        out_shape=jax.ShapeDtypeStruct(object_slices.shape, f32),
        in_specs=[vmem, vmem, pl.BlockSpec(memory_space=pltpu.SMEM), vmem, anywhere, anywhere],
        out_specs=vmem,
        scratch_shapes=[
            pltpu.VMEM((5, 2, rows, HALO), f32),
            pltpu.VMEM((5, 2, rows, HALO), f32),
            pltpu.VMEM((2, n, n), f32),
            pltpu.VMEM((2, n, n), f32),
            pltpu.VMEM((2, 2, n, n), f32),
            pltpu.VMEM((n, n), f32),
            pltpu.SMEM(positions.shape, jnp.int32),
            pltpu.VMEM(tables.shape, jnp.bfloat16),
            pltpu.VMEM(transfer.shape, f32),
            pltpu.VMEM((n, n), f32),
            pltpu.VMEM((n, n), f32),
            pltpu.VMEM((2, 2, n, HALO), f32),
            pltpu.VMEM((2, 2, n, HALO), f32),
            pltpu.VMEM((2, 2, 7, n + 2 * room, HALO), f32),
            pltpu.VMEM((2, 2, 7, n + 2 * room, HALO), f32),
            pltpu.VMEM((6, 2, rows, HALO), f32),
            pltpu.VMEM((2, 2, rows, HALO), f32),
            dma((2,)),
            dma((5,)),
            dma((2, 2, 2)),
            dma((2, 2)),
            dma((2, 4, 2)),
            dma((2,)),
            dma((3,)),
            dma((3,)),
            dma((2,)),
            dma((2, 2)),
            dma((3, 2)),
            dma((4, 2)),
            dma((2, 2)),
            dma((2, 2)),
            dma((2, 2)),
            dma((2, 2)),
        ],
        compiler_params=pltpu.CompilerParams(
            collective_id=0, has_side_effects=True, vmem_limit_bytes=60 * 1024 * 1024
        ),
    )(probe, object_slices, positions, measured, tables, transfer)


def solution(mesh):
    placed = (
        P("mode", None, None, None),
        P("depth", None, None, "tile"),
        P("tile", None),
        P("tile", None, None),
    )
    pairs = mesh.shape["tile"] // 2
    return jax.shard_map(
        functools.partial(body, pairs),
        mesh=mesh,
        in_specs=placed,
        out_specs=P("depth", None, None, "tile"),
        check_vma=False,
    )
```

```python
import functools
import math

import jax
import jax.numpy as jnp
import numpy as np
from jax import lax
from jax.experimental import pallas as pl
from jax.experimental.pallas import tpu as pltpu
from jax.sharding import PartitionSpec as P

HALO = 128
MESH = pl.DeviceIdType.MESH


def split_table(table):
    high = table.astype(jnp.bfloat16)
    low = (table - high.astype(np.float64)).astype(jnp.bfloat16)
    return np.stack([high, low], 0)


def dft_tables(length):
    ordinal = np.arange(length)
    angle = 2.0 * math.pi / length * (ordinal[:, None] * ordinal[None, :] % length)
    cosine = np.cos(angle) / math.sqrt(length)
    sine = np.sin(angle) / math.sqrt(length)
    first = np.block([[cosine, -sine], [sine, cosine]])
    second = np.block([[cosine, sine], [-sine, cosine]])
    return np.stack([split_table(first), split_table(second)], 0)


def propagator(length):
    ordinal = np.arange(length)
    signed = np.where(ordinal < length - length // 2, ordinal, ordinal - length)
    square = signed[:, None] * signed[:, None] + signed[None, :] * signed[None, :]
    angle = -math.pi / (2.0 * length) * (3 * square % (4 * length))
    return np.stack([np.cos(angle), np.sin(angle)], 0).astype(np.float32)


def parts_of(value):
    high = value.astype(jnp.bfloat16)
    low = (value - high.astype(jnp.float32)).astype(jnp.bfloat16)
    return high, low


def mm(a, b):
    return jnp.dot(a, b, preferred_element_type=jnp.float32)


def transform(real, imag, tab, right, left):
    n = real.shape[0]
    high, low = parts_of(jnp.concatenate([real, imag], axis=1))
    half = mm(high, tab[right, 0]) + mm(low, tab[right, 0]) + mm(high, tab[right, 1])
    high, low = parts_of(jnp.concatenate([half[:, :n], half[:, n:]], axis=0))
    full = mm(tab[left, 0], high) + mm(tab[left, 0], low) + mm(tab[left, 1], high)
    return full[:n], full[n:]


def kernel(
    pairs,
    probe_ref,
    obj_ref,
    pos_ref,
    meas_ref,
    tab_hbm,
    prop_hbm,
    out_ref,
    ext_near,
    ext_far,
    psi0,
    psi1,
    win,
    pattern,
    posn,
    tab,
    prop,
    mine_int,
    their_int,
    vsend,
    vrecv,
    spread_r,
    spread_i,
    accum,
    rim,
    load_sem,
    src_sem,
    fwd_sem,
    relay_sem,
    ext_sem,
    pos_sem,
    probe_sem,
    meas_sem,
    int_sem,
    v_sem,
    w_send,
    w_recv,
    rim_send,
    rim_recv,
    out_send,
    out_recv,
    own_sem,
):
    n = psi0.shape[1]
    rows = obj_ref.shape[2]
    room = rows - n
    d = lax.axis_index("depth")
    m = lax.axis_index("mode")
    t = lax.axis_index("tile")
    c = lax.rem(t, 2)
    z = t // 2
    other = t + 1 - 2 * c
    own = 1 - (c - d) * (c - d)
    core = {"tile": other}
    across = {"depth": 1 - d}
    beside = {"mode": 1 - m}
    is_owner = c == d
    not_owner = c != d

    def rcopy(src, dst, send, recv, target):
        return pltpu.make_async_remote_copy(
            src_ref=src, dst_ref=dst, send_sem=send, recv_sem=recv, device_id=target, device_id_type=MESH
        )

    loads = [
        pltpu.make_async_copy(tab_hbm, tab, load_sem.at[0]),
        pltpu.make_async_copy(prop_hbm, prop, load_sem.at[1]),
    ]
    for item in loads:
        item.start()

    barrier = pltpu.get_barrier_semaphore()
    for target in (core, across, beside):
        pl.semaphore_signal(barrier, inc=1, device_id=target, device_id_type=MESH)

    @pl.when(z > 0)
    def _():
        for depth in (0, 1):
            pl.semaphore_signal(barrier, inc=1, device_id={"depth": depth, "tile": t - 2}, device_id_type=MESH)

    @pl.when(z < pairs - 1)
    def _():
        for depth in (0, 1):
            pl.semaphore_signal(barrier, inc=1, device_id={"depth": depth, "tile": t + 2}, device_id_type=MESH)

    peers = 3 + 2 * jnp.minimum(z, 1) + 2 * jnp.minimum(pairs - 1 - z, 1)
    pl.semaphore_wait(barrier, peers)

    ext = (ext_near, ext_far)
    spread = (spread_r, spread_i)

    tall = rows // 2

    def strip(r):
        return pl.ds(pl.multiple_of(r * tall, 8), tall)

    def half_of(h, r):
        return obj_ref.at[0, :, strip(r), pl.ds(pl.multiple_of(h * HALO, HALO), HALO)]

    def slot(s, block, r):
        return ext[s].at[block, :, strip(r), :]

    def place(h, block, send, depth):
        for s in (0, 1):

            @pl.when(jnp.logical_and(d == s, depth == s))
            def _():
                for r in (0, 1):
                    pltpu.make_async_copy(half_of(h, r), slot(s, block, r), ext_sem.at[s, block, r]).start()

            @pl.when(jnp.logical_and(d == s, depth != s))
            def _():
                rcopy(half_of(h, m), slot(s, block, m), send, ext_sem.at[s, block, m], across).start()

    inner_block = 3 * c
    outer_block = 3 - 3 * c
    outer_tile = t - 2 + 4 * c
    has_outer = jnp.logical_or(jnp.logical_and(c == 0, z > 0), jnp.logical_and(c == 1, z < pairs - 1))

    def outer_copy(s, r):
        return rcopy(
            half_of(c, r),
            slot(s, outer_block, r),
            src_sem.at[3 + r],
            ext_sem.at[s, outer_block, r],
            {"depth": 1 - c, "tile": outer_tile},
        )

    pos_copy = rcopy(pos_ref, posn, pos_sem.at[0], pos_sem.at[1], core)
    pos_copy.start()
    place(0, 1, src_sem.at[0], c)
    place(1, 2, src_sem.at[1], c)
    place(1 - c, inner_block, src_sem.at[2], 1 - c)

    for s in (0, 1):

        @pl.when(jnp.logical_and(has_outer, d == s))
        def _():
            for r in (0, 1):
                outer_copy(s, r).start()

    probe_copy = rcopy(probe_ref.at[0], psi0, probe_sem.at[0], probe_sem.at[1], beside)

    @pl.when(c == m)
    def _():
        probe_copy.start()
        pltpu.make_async_copy(probe_ref.at[0], psi0, probe_sem.at[2]).start()

    meas_copy = rcopy(meas_ref.at[m], pattern, meas_sem.at[0], meas_sem.at[1], core)
    meas_local = pltpu.make_async_copy(meas_ref.at[m], pattern, meas_sem.at[2])

    @pl.when(is_owner)
    def _():
        meas_copy.start()
        meas_local.start()

    for s in (0, 1):
        ext[s][4] = jnp.zeros(ext_near.shape[1:], jnp.float32)

    no_left = jnp.logical_and(d == 0, z == 0)
    no_right = jnp.logical_and(d == 1, z == pairs - 1)

    @pl.when(no_left)
    def _():
        for s in (0, 1):
            ext[s][0] = jnp.zeros(ext_near.shape[1:], jnp.float32)

    @pl.when(no_right)
    def _():
        for s in (0, 1):
            ext[s][3] = jnp.zeros(ext_near.shape[1:], jnp.float32)

    @pl.when(is_owner)
    def _():
        @pl.loop(0, 4)
        def _(w):
            for field in spread:
                for j in (0, 1, 2, 5, 6):
                    field[w // 2, lax.rem(w, 2), j] = jnp.zeros(field.shape[3:], jnp.float32)
                for j in (3, 4):
                    for edge in (0, room + n):
                        field[w // 2, lax.rem(w, 2), j, edge : edge + room, :] = jnp.zeros((room, HALO), jnp.float32)

    def ext_wait(s, block, r):
        ref = slot(s, block, r)
        rcopy(ref, ref, src_sem.at[0], ext_sem.at[s, block, r], core).wait_recv()

    def forward_copy(s, i, block, r):
        ref = slot(s, block, r)
        return rcopy(ref, ref, fwd_sem.at[s, i, r], ext_sem.at[s, block, r], core)

    def relay_copy(s, i, block):
        ref = slot(s, block, m)
        return rcopy(ref, ref, relay_sem.at[s, i], ext_sem.at[s, block, m], beside)

    def missing(i):
        return no_left if i == 0 else no_right

    def lands(i):
        return jnp.logical_and(not_owner, jnp.logical_not(missing(i)))

    def relays(s, i):
        return jnp.logical_and(d != s, jnp.logical_and(not_owner, d != i))

    def land(s, second):
        r = 1 - m if second else m
        for i in (0, 1):

            @pl.when(is_owner)
            def _():
                ext_wait(s, 1 + i, r)
                forward_copy(s, i, 1 + i, r).start()

            @pl.when(lands(i))
            def _():
                ext_wait(s, 3 * i, r)
                forward_copy(s, i, 3 * i, r).start()

            if not second:

                @pl.when(jnp.logical_and(is_owner, d != s))
                def _():
                    relay_copy(s, i, 1 + i).start()

                @pl.when(relays(s, i))
                def _():
                    relay_copy(s, i, 3 * i).start()

    def arrive(s):
        for i in (0, 1):
            for r in (0, 1):

                @pl.when(not_owner)
                def _():
                    ext_wait(s, 1 + i, r)

                @pl.when(jnp.logical_and(is_owner, jnp.logical_not(missing(i))))
                def _():
                    ext_wait(s, 3 * i, r)

    lane = lax.broadcasted_iota(jnp.int32, (1, HALO), 1)

    def place_of(tile_no, which):
        mine = tile_no == c
        top = jnp.where(mine, pos_ref[which, 0], posn[which, 0])
        left = jnp.where(mine, pos_ref[which, 1], posn[which, 1])
        return top, left // HALO, lax.rem(left, HALO)

    def cut(s, spot):
        top, block, rem = spot
        back = lax.rem(HALO - rem, HALO)
        for part in (0, 1):
            for j in (0, 1):
                near = ext[s][block + j, part, pl.ds(top, n), :]
                far = ext[s][block + j + 1, part, pl.ds(top, n), :]
                mixed = jnp.where(lane >= rem, near, far)
                win[s, part, :, j * HALO : (j + 1) * HALO] = pltpu.roll(mixed, back, 1)

    @pl.when(d == 1)
    def _():
        land(1, False)
        land(1, True)

    land(0, False)
    land(0, True)

    @pl.when(d == 0)
    def _():
        land(1, False)

    for item in loads:
        item.wait()
    pos_copy.wait()

    @pl.when(c == m)
    def _():
        pltpu.make_async_copy(probe_ref.at[0], psi0, probe_sem.at[2]).wait()

    @pl.when(c != m)
    def _():
        probe_copy.wait_recv()

    spot = place_of(d, m)
    arrive(0)
    cut(0, spot)
    wr, wi = win[0, 0], win[0, 1]
    pr, pi = psi0[0], psi0[1]
    spec_r, spec_i = transform(pr * wr - pi * wi, pr * wi + pi * wr, tab, 0, 1)
    hr, hi = prop[0], prop[1]
    wave_r, wave_i = transform(spec_r * hr - spec_i * hi, spec_r * hi + spec_i * hr, tab, 1, 0)
    psi1[0] = wave_r
    psi1[1] = wave_i

    @pl.when(d == 0)
    def _():
        land(1, True)

    arrive(1)
    cut(1, spot)
    wr, wi = win[1, 0], win[1, 1]
    wave_r, wave_i = psi1[0], psi1[1]
    far_r, far_i = transform(wave_r * wr - wave_i * wi, wave_r * wi + wave_i * wr, tab, 0, 1)
    mine_int[...] = far_r * far_r + far_i * far_i
    int_copy = rcopy(mine_int, their_int, int_sem.at[0], int_sem.at[1], core)
    int_copy.start()

    @pl.when(is_owner)
    def _():
        meas_local.wait()

    @pl.when(not_owner)
    def _():
        meas_copy.wait_recv()

    int_copy.wait()
    resid = mine_int[...] + their_int[...] - pattern[...]
    q_r, q_i = transform(resid * far_r, resid * far_i, tab, 1, 0)

    def v_copy(part):
        return rcopy(vsend.at[part], vrecv.at[part], v_sem.at[0, part], v_sem.at[1, part], core)

    def window_at(tile_no, which, part):
        return spread[part].at[tile_no, which, 3:5, room : room + n, :]

    def give(real, imag):
        for part, value in enumerate((real, imag)):
            for j in (0, 1):
                vsend[part, j] = value[:, j * HALO : (j + 1) * HALO]
            v_copy(part).start()

    def keep(real, imag):
        for part, value in enumerate((real, imag)):
            for j in (0, 1):
                spread[part][d, m, 3 + j, room : room + n, :] = value[:, j * HALO : (j + 1) * HALO]

    def carry(tile_no, which, part, k, j, target):
        ref = window_at(tile_no, which, part)
        return rcopy(ref, ref, w_send.at[k, part], w_recv.at[j, part], target)

    def to_across(part):
        return carry(d, m, part, 0, 0, across)

    def to_beside(part):
        return carry(d, m, part, 1, 1, beside)

    def aside():
        return carry(d, m, 1, 1, 3, beside)

    def relay_beside():
        return carry(1 - d, m, 0, 2, 2, beside)

    def relay_across():
        return carry(d, 1 - m, 1, 2, 2, across)

    def finish():
        for part in (0, 1):
            v_copy(part).wait_recv()
            here = window_at(d, m, part)
            here[...] = here[...] + vrecv[part]

            @pl.when(is_owner)
            def _():
                to_beside(part).start()

            @pl.when(not_owner)
            def _():
                if part == 1:
                    aside().start()
                to_across(part).start()

    wr, wi = win[1, 0], win[1, 1]
    wave_r, wave_i = psi1[0], psi1[1]
    v_r = wave_r * q_r + wave_i * q_i
    v_i = wave_r * q_i - wave_i * q_r

    @pl.when(c == 0)
    def _():
        give(v_r, v_i)

    @pl.when(c == 1)
    def _():
        keep(v_r, v_i)

    spec_r, spec_i = transform(wr * q_r + wi * q_i, wr * q_i - wi * q_r, tab, 0, 1)

    @pl.when(c == 1)
    def _():
        finish()

    hr, hi = prop[0], prop[1]
    q_r, q_i = transform(spec_r * hr + spec_i * hi, spec_i * hr - spec_r * hi, tab, 1, 0)
    pr, pi = psi0[0], psi0[1]
    v_r = pr * q_r + pi * q_i
    v_i = pr * q_i - pi * q_r

    @pl.when(c == 1)
    def _():
        give(v_r, v_i)

    @pl.when(c == 0)
    def _():
        keep(v_r, v_i)
        finish()

    def placed(tile_no, which, block, part):
        top, first, rem = place_of(tile_no, which)
        at = block - first + 3
        near = spread[part][tile_no, which, at, pl.ds(room - top, rows), :]
        far = spread[part][tile_no, which, at - 1, pl.ds(room - top, rows), :]
        return pltpu.roll(jnp.where(lane < HALO - rem, near, far), rem, 1)

    def gather_block(block, part):
        terms = []
        for tile_no in (0, 1):
            local = block - 2 * tile_no
            if 0 <= local < 4:
                for which in (0, 1):
                    terms.append(placed(tile_no, which, local, part))
        accum[block, part] = functools.reduce(jnp.add, terms)

    def rim_copy(side, part):
        return rcopy(
            accum.at[5 * side, part],
            rim.at[1 - side, part],
            rim_send.at[side, part],
            rim_recv.at[1 - side, part],
            {"tile": t - 2 + 4 * side},
        )

    def out_copy(outer, part):
        half = d * (1 - outer) + (1 - d) * outer
        block = 3 - 2 * d + half
        return rcopy(
            accum.at[block, part],
            out_ref.at[0, part, :, pl.ds(pl.multiple_of(half * HALO, HALO), HALO)],
            out_send.at[outer, part],
            out_recv.at[outer, part],
            core,
        )

    def own_copy(outer, part):
        half = (1 - d) * (1 - outer) + d * outer
        return pltpu.make_async_copy(
            accum.at[1 + 2 * d + half, part],
            out_ref.at[0, part, :, pl.ds(pl.multiple_of(half * HALO, HALO), HALO)],
            own_sem.at[outer, part],
        )

    has_low = z > 0
    has_high = z < pairs - 1

    @pl.when(is_owner)
    def _():
        carry(1 - d, m, 0, 2, 0, across).wait_recv()
        relay_beside().start()
        for part in (0, 1):
            if part == 1:
                carry(1 - d, m, 1, 2, 0, across).wait_recv()
            carry(d, 1 - m, part, 2, 1, beside).wait_recv()
            carry(1 - d, 1 - m, part, 2, 2, beside).wait_recv()
            gather_block(0, part)

            @pl.when(has_low)
            def _():
                rim_copy(0, part).start()

            gather_block(5, part)

            @pl.when(has_high)
            def _():
                rim_copy(1, part).start()

            for block in (2, 3):
                gather_block(block, part)
            out_copy(0, part).start()
            own_copy(0, part).start()
            for block in (1, 4):
                gather_block(block, part)
        for part in (0, 1):
            for side, block, there in ((0, 1, has_low), (1, 4, has_high)):

                @pl.when(there)
                def _():
                    rcopy(
                        rim.at[side, part], rim.at[side, part], rim_send.at[side, part], rim_recv.at[side, part], core
                    ).wait_recv()
                    accum[block, part] = accum[block, part] + rim[side, part]

            out_copy(1, part).start()
            own_copy(1, part).start()
        relay_beside().wait_send()
        for part in (0, 1):
            to_beside(part).wait_send()
            for outer in (0, 1):
                out_copy(outer, part).wait_send()
                own_copy(outer, part).wait()
            for side, there in ((0, has_low), (1, has_high)):

                @pl.when(there)
                def _():
                    rim_copy(side, part).wait_send()

        meas_copy.wait_send()

    @pl.when(not_owner)
    def _():
        carry(d, 1 - m, 1, 2, 3, beside).wait_recv()
        relay_across().start()
        for part in (0, 1):
            to_across(part).wait_send()
        aside().wait_send()
        relay_across().wait_send()
        for part in (0, 1):
            for outer in (0, 1):
                out_copy(outer, part).wait_recv()

    for part in (0, 1):
        v_copy(part).wait_send()

    @pl.when(c == m)
    def _():
        probe_copy.wait_send()

    def placed_done(h, block, send, depth):
        @pl.when(d != depth)
        def _():
            rcopy(half_of(h, m), slot(0, block, m), send, ext_sem.at[0, block, m], across).wait_send()

    placed_done(0, 1, src_sem.at[0], c)
    placed_done(1, 2, src_sem.at[1], c)
    placed_done(1 - c, inner_block, src_sem.at[2], 1 - c)

    @pl.when(has_outer)
    def _():
        for r in (0, 1):
            outer_copy(0, r).wait_send()

    for s in (0, 1):
        for i in (0, 1):

            @pl.when(is_owner)
            def _():
                for r in (0, 1):
                    forward_copy(s, i, 1 + i, r).wait_send()

            @pl.when(lands(i))
            def _():
                for r in (0, 1):
                    forward_copy(s, i, 3 * i, r).wait_send()

            @pl.when(jnp.logical_and(is_owner, d != s))
            def _():
                relay_copy(s, i, 1 + i).wait_send()

            @pl.when(relays(s, i))
            def _():
                relay_copy(s, i, 3 * i).wait_send()


def body(pairs, probe, object_slices, positions, measured):
    n = probe.shape[-1]
    rows = object_slices.shape[2]
    room = rows - n
    f32 = jnp.float32
    tables = jnp.asarray(dft_tables(n))
    transfer = jnp.asarray(propagator(n))
    vmem = pl.BlockSpec(memory_space=pltpu.VMEM)
    anywhere = pl.BlockSpec(memory_space=pl.ANY)
    dma = pltpu.SemaphoreType.DMA
    return pl.pallas_call(
        functools.partial(kernel, pairs),
        out_shape=jax.ShapeDtypeStruct(object_slices.shape, f32),
        in_specs=[vmem, vmem, pl.BlockSpec(memory_space=pltpu.SMEM), vmem, anywhere, anywhere],
        out_specs=anywhere,
        scratch_shapes=[
            pltpu.VMEM((5, 2, rows, HALO), f32),
            pltpu.VMEM((5, 2, rows, HALO), f32),
            pltpu.VMEM((2, n, n), f32),
            pltpu.VMEM((2, n, n), f32),
            pltpu.VMEM((2, 2, n, n), f32),
            pltpu.VMEM((n, n), f32),
            pltpu.SMEM(positions.shape, jnp.int32),
            pltpu.VMEM(tables.shape, jnp.bfloat16),
            pltpu.VMEM(transfer.shape, f32),
            pltpu.VMEM((n, n), f32),
            pltpu.VMEM((n, n), f32),
            pltpu.VMEM((2, 2, n, HALO), f32),
            pltpu.VMEM((2, 2, n, HALO), f32),
            pltpu.VMEM((2, 2, 7, n + 2 * room, HALO), f32),
            pltpu.VMEM((2, 2, 7, n + 2 * room, HALO), f32),
            pltpu.VMEM((6, 2, rows, HALO), f32),
            pltpu.VMEM((2, 2, rows, HALO), f32),
            dma((2,)),
            dma((5,)),
            dma((2, 2, 2)),
            dma((2, 2)),
            dma((2, 4, 2)),
            dma((2,)),
            dma((3,)),
            dma((3,)),
            dma((2,)),
            dma((2, 2)),
            dma((3, 2)),
            dma((4, 2)),
            dma((2, 2)),
            dma((2, 2)),
            dma((2, 2)),
            dma((2, 2)),
            dma((2, 2)),
        ],
        compiler_params=pltpu.CompilerParams(
            collective_id=0, has_side_effects=True, vmem_limit_bytes=60 * 1024 * 1024
        ),
    )(probe, object_slices, positions, measured, tables, transfer)


def solution(mesh):
    placed = (
        P("mode", None, None, None),
        P("depth", None, None, "tile"),
        P("tile", None),
        P("tile", None, None),
    )
    pairs = mesh.shape["tile"] // 2
    return jax.shard_map(
        functools.partial(body, pairs),
        mesh=mesh,
        in_specs=placed,
        out_specs=P("depth", None, None, "tile"),
        check_vma=False,
    )
```
